32 devices in a mesh: frag: 4 (over y, core), band: 8 (over z, x).
Axes of the slice: x: 2, y: 2, z: 4, core: 2. Of those that a mesh axis runs over, the one named last changes fastest.
Arguments:
- wave_coeffs: bfloat16 [4, 256, 262144], P('frag', 'band'), may hold values from -40 to 40
- old_potential: float32 [4, 262144], P('frag'), may hold values from -4 to 4
- occupations: float32 [4, 256], P('frag'), may hold values from 0 to 2
- box_sizes: int32 [4, 3], replicated, may hold values from 32 to 64, as said below
- box_offsets: int32 [4, 3], replicated, may hold values from 0 to 96, as said below
- patch_signs: int32 [4], replicated, may hold values from -1 to 1, as said below
Outputs:
- new_waves: bfloat16 [4, 256, 262144], P('frag', 'band')
- box_potential: float32 [4, 262144], P('frag')
- total_potential: float32 [128, 128, 128], P('band')
The draws below stay inside these ranges and needn't reach their ends.
Inputs may be any that keep to these rules, and one draw needn't show every extreme that they name: `box_sizes`: each entry is 32, 48 or 64. box_offsets + box_sizes <= 128 in every dimension. `patch_signs`: each entry is -1 or 1.
All inputs are finite; a program needn't handle non-finite values.
Results may differ from the reference program's by a relative error of at most 0.0065.
Values may be sent and summed in bfloat16 or wider, within the bound.
A program may use at most 384 MiB of HBM per device.

```python
import jax
import jax.numpy as jnp
from jax import lax

NB = 256
BOX = 64
G = 128
NS_ITERS = 8
FRAGS = 4
N_BAND = 8


def box_layout(key):
    size_key = jax.random.fold_in(key, 11)
    offset_key = jax.random.fold_in(key, 12)
    levels = jax.random.randint(size_key, (FRAGS, 3), 0, 3)
    levels = levels.at[0, :].set(2)
    levels = levels.at[1, :].set(0)
    levels = levels.at[2, 0].set(0)
    box_sizes = BOX // 4 * (2 + levels)
    raw_offsets = jax.random.randint(offset_key, (FRAGS, 3), 0, G - BOX // 2 + 1)
    offsets = raw_offsets % (G - box_sizes + 1)
    offsets = offsets.at[0, 0].set(0)
    offsets = offsets.at[1, 0].set(G - BOX // 2)
    offsets = offsets.at[2, 0].set(G // N_BAND)
    return (box_sizes.astype(jnp.int32), offsets.astype(jnp.int32))


def draw_box_sizes(key, part):
    return box_layout(key)[0]


def draw_box_offsets(key, part):
    return box_layout(key)[1]


def draw_patch_signs(key, part):
    signs = 2 * jax.random.randint(jax.random.fold_in(key, 21), (FRAGS,), 0, 2) - 1
    signs = signs.at[0].set(1)
    signs = signs.at[1].set(-1)
    return signs.astype(jnp.int32)


def draw_wave_coeffs(key, part):
    scale_key = jax.random.fold_in(key, 31)
    value_key = jax.random.fold_in(key, 32)
    scales = jnp.exp(jax.random.uniform(scale_key, (FRAGS, NB, 1), jnp.float32, 0.0, jnp.log(10.0)))
    values = scales * jnp.clip(jax.random.normal(value_key, (FRAGS, NB, BOX ** 3), jnp.float32), -4.0, 4.0)
    return values.astype(jnp.bfloat16)


def level_of(own_key, extent, shards, least, largest):
    factor_of = 1.0
    for axis_at, blocks in shards:
        heights = jax.random.uniform(jax.random.fold_in(jax.random.fold_in(own_key, 6), axis_at), (blocks,), jnp.float32, least / len(shards), largest / len(shards))
        factor_of = factor_of * jnp.repeat(jnp.exp(heights), extent[axis_at] // blocks).reshape((-1,) + (1,) * (len(extent) - 1 - axis_at))
    return factor_of


def noise(own_key, shape, deviation, reach, shards=(), kind=jnp.bfloat16):
    entries = deviation * jax.random.normal(own_key, shape, jnp.float32)
    if shards:
        entries = entries * level_of(own_key, shape, shards, -0.22, 0.18)
    return jnp.clip(entries, -reach, reach).astype(kind)


def setup_inputs(seed: int = 0) -> dict:
    seeds = jax.random.split(jax.random.key(seed), 7)
    wave_coeffs = draw_wave_coeffs(jax.random.fold_in(seeds[6], 71), 0)
    old_potential = noise(seeds[1], (FRAGS, BOX**3), 1.0, 4.0, ((0, 4),), jnp.float32)
    occupations = jnp.clip(2.0 * jax.random.uniform(seeds[2], (FRAGS, NB), jnp.float32) ** level_of(seeds[2], (FRAGS, NB), ((0, 4),), -0.2, 0.2), 0.0, 2.0)
    box_sizes = draw_box_sizes(jax.random.fold_in(seeds[6], 71), 0)
    box_offsets = draw_box_offsets(jax.random.fold_in(seeds[6], 71), 0)
    patch_signs = draw_patch_signs(jax.random.fold_in(seeds[6], 71), 0)
    return {"wave_coeffs": wave_coeffs, "old_potential": old_potential, "occupations": occupations, "box_sizes": box_sizes, "box_offsets": box_offsets, "patch_signs": patch_signs}


step_size = 0.1
screening = 0.5
local_factor = 0.75
epsilon = 1e-06

def box_mask(box_size):
    coords = jnp.arange(BOX).astype(jnp.int32)
    along_x = (coords < box_size[0]).astype(jnp.float32)
    along_y = (coords < box_size[1]).astype(jnp.float32)
    along_z = (coords < box_size[2]).astype(jnp.float32)
    return (along_x[:, None, None] * along_y[None, :, None] * along_z[None, None, :]).reshape(BOX * BOX * BOX)

def sine_table():
    index = jnp.arange(G).astype(jnp.float32) + 1.0
    table = jnp.sqrt(2.0 / (G + 1)) * jnp.sin(jnp.pi * index[:, None] * index[None, :] / (G + 1))
    eigen = 2.0 - 2.0 * jnp.cos(jnp.pi * index / (G + 1))
    return (table, eigen)

def newton_schulz(gram):
    highest = lax.Precision.HIGHEST
    frobenius = jnp.sqrt(jnp.sum(gram * gram) + epsilon)
    identity = jnp.eye(NB, dtype=jnp.float32)
    square_part = gram / frobenius
    inverse_part = identity
    for sweep in range(NS_ITERS):
        newton_step = 0.5 * (3.0 * identity - jnp.dot(inverse_part, square_part, precision=highest, preferred_element_type=jnp.float32))
        square_part = jnp.dot(square_part, newton_step, precision=highest, preferred_element_type=jnp.float32)
        inverse_part = jnp.dot(newton_step, inverse_part, precision=highest, preferred_element_type=jnp.float32)
    return (inverse_part / jnp.sqrt(frobenius)).astype(jnp.bfloat16)

def reference(wave_coeffs, old_potential, occupations, box_sizes, box_offsets, patch_signs):
    highest = lax.Precision.HIGHEST
    cell_volume = 1.0 / BOX ** 3
    table, eigen = sine_table()
    fresh_list = []
    patched = jnp.zeros((G, G, G), jnp.float32)
    for fragment in range(FRAGS):
        mask = box_mask(box_sizes[fragment])
        waves = wave_coeffs[fragment].astype(jnp.float32) * mask[None, :]
        cube = waves.reshape(NB, BOX, BOX, BOX)
        padded = jnp.pad(cube, ((0, 0), (1, 1), (1, 1), (1, 1)))
        beside = padded[:, 2:, 1:-1, 1:-1] + padded[:, :-2, 1:-1, 1:-1]
        beside = beside + padded[:, 1:-1, 2:, 1:-1] + padded[:, 1:-1, :-2, 1:-1]
        beside = beside + padded[:, 1:-1, 1:-1, 2:] + padded[:, 1:-1, 1:-1, :-2]
        kinetic = (6.0 * cube - beside).reshape(NB, BOX * BOX * BOX)
        applied = 0.5 * kinetic + old_potential[fragment][None, :] * waves
        trial = (mask[None, :] * (waves - step_size * applied)).astype(jnp.bfloat16)
        gram = lax.dot_general(trial, trial, (((1,), (1,)), ((), ())), preferred_element_type=jnp.float32) * cell_volume
        coeff = newton_schulz(gram)
        fresh = lax.dot_general(coeff, trial, (((0,), (0,)), ((), ())), preferred_element_type=jnp.float32)
        fresh_list.append(fresh.astype(jnp.bfloat16))
        density = lax.optimization_barrier(jnp.sum(occupations[fragment][:, None] * fresh * fresh, axis=0)) / NB
        frame = jnp.zeros((G + BOX, G + BOX, G + BOX), jnp.float32)
        start = box_offsets[fragment].astype(jnp.int32)
        frame = lax.dynamic_update_slice(frame, density.reshape(BOX, BOX, BOX), (start[0], start[1], start[2]))
        patched = patched + patch_signs[fragment].astype(jnp.float32) * frame[:G, :G, :G]
    spectrum = jnp.einsum('abc,ci->abi', patched, table, precision=highest)
    spectrum = jnp.einsum('abc,bi->aic', spectrum, table, precision=highest)
    spectrum = jnp.einsum('abc,ai->ibc', spectrum, table, precision=highest)
    spectrum = spectrum * (screening / (eigen[:, None, None] + eigen[None, :, None] + eigen[None, None, :] + screening))
    spectrum = jnp.einsum('abc,ai->ibc', spectrum, table, precision=highest)
    spectrum = jnp.einsum('abc,bi->aic', spectrum, table, precision=highest)
    hartree = jnp.einsum('abc,ci->abi', spectrum, table, precision=highest)
    total_potential = hartree - local_factor * jnp.cbrt(jnp.maximum(patched, 0.0))
    extended = jnp.pad(total_potential, ((0, BOX), (0, BOX), (0, BOX)))
    windows = []
    for fragment in range(FRAGS):
        mask = box_mask(box_sizes[fragment])
        start = box_offsets[fragment].astype(jnp.int32)
        window = lax.dynamic_slice(extended, (start[0], start[1], start[2]), (BOX, BOX, BOX))
        windows.append(window.reshape(BOX * BOX * BOX) * mask)
    return (jnp.stack(fresh_list), jnp.stack(windows), total_potential)
```

```python
import functools

import jax
import jax.numpy as jnp
from jax import lax
from jax.experimental import pallas as pl
from jax.experimental.pallas import tpu as pltpu
from jax.sharding import PartitionSpec as P

NB = 256
BOX = 64
G = 128
NS_ITERS = 8


step_size = 0.1
screening = 0.5
local_factor = 0.75
epsilon = 1e-06


def sine_table():
    index = jnp.arange(G).astype(jnp.float32) + 1.0
    table = jnp.sqrt(2.0 / (G + 1)) * jnp.sin(jnp.pi * index[:, None] * index[None, :] / (G + 1))
    eigen = 2.0 - 2.0 * jnp.cos(jnp.pi * index / (G + 1))
    return (table, eigen)


def newton_schulz(gram):
    highest = lax.Precision.HIGHEST
    frobenius = jnp.sqrt(jnp.sum(gram * gram) + epsilon)
    identity = jnp.eye(NB, dtype=jnp.float32)
    square_part = gram / frobenius
    inverse_part = identity
    for sweep in range(NS_ITERS):
        newton_step = 0.5 * (
            3.0 * identity
            - jnp.dot(
                inverse_part, square_part, precision=highest, preferred_element_type=jnp.float32
            )
        )
        square_part = jnp.dot(
            square_part, newton_step, precision=highest, preferred_element_type=jnp.float32
        )
        inverse_part = jnp.dot(
            newton_step, inverse_part, precision=highest, preferred_element_type=jnp.float32
        )
    return (inverse_part / jnp.sqrt(frobenius)).astype(jnp.bfloat16)


GROUP = 8 * BOX
LANES = 128


def step_plan(band_count):
    return (2, 1) if 16 % band_count == 0 else (1, 2)


def live_units(sizes, band_count):
    planes, parts = step_plan(band_count)
    unit = jnp.arange(BOX // planes * parts, dtype=jnp.int32)
    per_device = sizes[0] * parts // (planes * band_count)
    owner = jnp.minimum(unit // per_device, band_count - 1)
    return (owner, unit % per_device)


def trial_kernel(planes, parts, sizes, owner, local, prev, main, after, potential, out):
    step, part = pl.program_id(0), pl.program_id(1)
    size_x, size_y, size_z = sizes[0], sizes[1], sizes[2]
    plane_cells = BOX * BOX
    place = local[step * parts + part]
    groups = size_y // (8 * parts)
    rows = out.shape[1]
    band_rows = min(rows, 16)
    z = lax.rem(lax.broadcasted_iota(jnp.int32, (band_rows, LANES), 1), BOX)
    low_half = lax.broadcasted_iota(jnp.int32, (band_rows, LANES), 1) < BOX
    alive = z < size_z
    has_up = z < size_z - 1
    has_down = z > 0
    weight = jnp.where(alive, 0.5 * step_size, 0.0)

    @pl.when(step * planes < size_x)
    def _():
        for p in range(planes):
            x = step * planes + p
            below, below_at = (prev, 0) if p == 0 else (main, (p - 1) * plane_cells)
            above, above_at = (after, 0) if p == planes - 1 else (main, (p + 1) * plane_cells)
            below_on = jnp.where(x > 0, 1.0, 0.0)
            above_on = jnp.where(x + 1 < size_x, 1.0, 0.0)

            def group_step(local_group, carry):
                group = part * groups + local_group
                base = group * GROUP
                target = ((place * planes + p) * groups + local_group) * (8 * size_z)
                head_on = jnp.where(group > 0, 1.0, 0.0)
                tail_on = jnp.where(group * 8 + 8 < size_y, 1.0, 0.0)
                for first in range(0, rows, band_rows):
                    band = slice(first, first + band_rows)

                    def load(ref, at):
                        return ref[band, pl.ds(pl.multiple_of(at, LANES), LANES)].astype(
                            jnp.float32
                        )

                    def store(k, value):
                        at = pl.multiple_of(target + k * LANES, LANES)
                        out[0, band, pl.ds(at, LANES)] = value.astype(out.dtype)

                    here = [load(main, p * plane_cells + base + k * LANES) for k in range(4)]
                    head = load(main, p * plane_cells + jnp.maximum(base - LANES, 0)) * head_on
                    tail = (
                        load(main, p * plane_cells + jnp.minimum(base + GROUP, plane_cells - LANES))
                        * tail_on
                    )
                    turned = [pltpu.roll(v, BOX, 1) for v in [head] + here + [tail]]
                    trial = []
                    for k in range(4):
                        v = here[k]
                        at = base + k * LANES
                        beside = jnp.where(has_up, pltpu.roll(v, LANES - 1, 1), 0.0)
                        beside = beside + jnp.where(has_down, pltpu.roll(v, 1, 1), 0.0)
                        beside = beside + turned[k + 1]
                        beside = beside + jnp.where(low_half, turned[k], turned[k + 2])
                        beside = beside + below_on * load(below, below_at + at)
                        beside = beside + above_on * load(above, above_at + at)
                        pot = potential[
                            0:1, pl.ds(pl.multiple_of(p * plane_cells + at, LANES), LANES)
                        ]
                        own = jnp.where(alive, (1.0 - 3.0 * step_size) - step_size * pot, 0.0)
                        trial.append(own * v + weight * beside)

                    @pl.when(size_z == 64)
                    def _():
                        for k in range(4):
                            store(k, trial[k])

                    @pl.when(size_z == 48)
                    def _():
                        for k in range(3):
                            filler = pltpu.roll(trial[3], 48 - 16 * k, 1)
                            store(k, jnp.where(z < 48, trial[k], filler))

                    @pl.when(size_z == 32)
                    def _():
                        for k in range(2):
                            filler = pltpu.roll(trial[2 * k + 1], 32, 1)
                            store(k, jnp.where(z < 32, trial[2 * k], filler))

                return carry

            lax.fori_loop(0, groups, group_step, 0)


def packed_trial(wave, potential, sizes, owner, local, width, band_count):
    rows = wave.shape[0]
    planes, parts = step_plan(band_count)
    plane_cells = BOX * BOX

    def plane(step, sizes, shift):
        return jnp.clip(step * planes + shift, 0, sizes[0] - 1)

    def whole(i, j, sizes, owner, local):
        return (0, jnp.minimum(i, sizes[0] // planes - 1))

    return pl.pallas_call(
        functools.partial(trial_kernel, planes, parts),
        out_shape=jax.ShapeDtypeStruct((band_count, rows, width), jnp.bfloat16),
        grid_spec=pltpu.PrefetchScalarGridSpec(
            num_scalar_prefetch=3,
            grid=(BOX // planes, parts),
            in_specs=[
                pl.BlockSpec((rows, plane_cells), lambda i, j, s, o, l: (0, plane(i, s, -1))),
                pl.BlockSpec((rows, planes * plane_cells), whole),
                pl.BlockSpec((rows, plane_cells), lambda i, j, s, o, l: (0, plane(i, s, planes))),
                pl.BlockSpec((1, planes * plane_cells), whole),
            ],
            out_specs=pl.BlockSpec(
                (1, rows, width), lambda i, j, s, o, l: (o[i * parts + j], 0, 0)
            ),
        ),
        compiler_params=pltpu.CompilerParams(vmem_limit_bytes=40 << 20),
        name="packed_trial",
    )(sizes, owner, local, wave, wave, wave, potential)


def unpack_kernel(planes, parts, sizes, owner, local, packed, out):
    step, part = pl.program_id(0), pl.program_id(1)
    size_x, size_y, size_z = sizes[0], sizes[1], sizes[2]
    plane_cells = BOX * BOX
    place = local[step * parts + part]
    groups = size_y // (8 * parts)
    rows = out.shape[0]
    band_rows = min(rows, 16)
    z = lax.rem(lax.broadcasted_iota(jnp.int32, (band_rows, LANES), 1), BOX)

    @pl.when((part == 0) & ((size_y < BOX) | (step * planes >= size_x)))
    def _():
        def clear(k, carry):
            out[:, pl.ds(pl.multiple_of(k * GROUP, GROUP), GROUP)] = jnp.zeros(
                (rows, GROUP), out.dtype
            )
            return carry

        lax.fori_loop(0, planes * plane_cells // GROUP, clear, 0)

    @pl.when(step * planes < size_x)
    def _():
        for p in range(planes):

            def group_step(local_group, carry):
                base = p * plane_cells + (part * groups + local_group) * GROUP
                source = ((place * planes + p) * groups + local_group) * (8 * size_z)
                for first in range(0, rows, band_rows):
                    band = slice(first, first + band_rows)

                    def load(k):
                        at = pl.multiple_of(source + k * LANES, LANES)
                        return packed[0, band, pl.ds(at, LANES)].astype(jnp.float32)

                    def store(k, value):
                        at = pl.multiple_of(base + k * LANES, LANES)
                        out[band, pl.ds(at, LANES)] = value.astype(out.dtype)

                    @pl.when(size_z == 64)
                    def _():
                        for k in range(4):
                            store(k, load(k))

                    @pl.when(size_z == 48)
                    def _():
                        last = jnp.zeros((band_rows, LANES), jnp.float32)
                        for k in range(3):
                            value = load(k)
                            store(k, jnp.where(z < 48, value, 0.0))
                            mine = (z >= 16 * k) & (z < 16 * k + 16)
                            last = jnp.where(mine, pltpu.roll(value, 80 + 16 * k, 1), last)
                        store(3, last)

                    @pl.when(size_z == 32)
                    def _():
                        for k in range(2):
                            value = load(k)
                            store(2 * k, jnp.where(z < 32, value, 0.0))
                            store(2 * k + 1, jnp.where(z < 32, pltpu.roll(value, 96, 1), 0.0))

                return carry

            lax.fori_loop(0, groups, group_step, 0)


def unpacked(packed, sizes, owner, local):
    band_count, rows, width = packed.shape
    planes, parts = step_plan(band_count)
    return pl.pallas_call(
        functools.partial(unpack_kernel, planes, parts),
        out_shape=jax.ShapeDtypeStruct((rows, BOX**3), packed.dtype),
        grid_spec=pltpu.PrefetchScalarGridSpec(
            num_scalar_prefetch=3,
            grid=(BOX // planes, parts),
            in_specs=[
                pl.BlockSpec((1, rows, width), lambda i, j, s, o, l: (o[i * parts + j], 0, 0))
            ],
            out_specs=pl.BlockSpec((rows, planes * BOX * BOX), lambda i, j, s, o, l: (0, i)),
        ),
        compiler_params=pltpu.CompilerParams(vmem_limit_bytes=40 << 20),
        name="unpacked",
    )(sizes, owner, local, packed)


def summed(partial_value, band_count):
    blocks = partial_value.reshape(band_count, NB // band_count, NB)
    blocks = lax.all_to_all(blocks, "band", split_axis=0, concat_axis=0, tiled=True)
    mine = jnp.sum(blocks, axis=0)
    return gathered(mine, band_count).reshape(NB, NB)


def gathered(block, band_count):
    copies = jnp.broadcast_to(block[None], (band_count,) + block.shape)
    return lax.all_to_all(copies, "band", split_axis=0, concat_axis=0, tiled=True)


def body(wave_coeffs, old_potential, occupations, box_sizes, box_offsets, patch_signs):
    highest = lax.Precision.HIGHEST
    fragment = lax.axis_index("frag")
    band_index = lax.axis_index("band")
    band_count = lax.axis_size("band")
    cells = BOX * BOX * BOX
    cell_volume = 1.0 / BOX**3
    zero_index = jnp.zeros((), jnp.int32)
    sizes_here = lax.dynamic_index_in_dim(box_sizes, fragment, 0, keepdims=False)
    offsets_here = lax.dynamic_index_in_dim(box_offsets, fragment, 0, keepdims=False)
    sign_here = lax.dynamic_index_in_dim(patch_signs, fragment, 0, keepdims=False)
    position = jnp.arange(cells)
    x_coord = position // (BOX * BOX)
    y_coord = position // BOX % BOX
    z_coord = position % BOX
    mask = (
        (x_coord < sizes_here[0]) & (y_coord < sizes_here[1]) & (z_coord < sizes_here[2])
    ).astype(jnp.float32)
    owner, local = live_units(sizes_here, band_count)
    room = cells // band_count
    lengths = (BOX // 2, BOX * 3 // 4, BOX)
    widths = sorted({a * b * c // band_count for a in lengths for b in lengths for c in lengths})
    width_here = sizes_here[0] * sizes_here[1] * sizes_here[2] // band_count
    choice = jnp.sum((width_here > jnp.array(widths)).astype(jnp.int32))

    def forward(width):
        def branch(wave, potential):
            trial = packed_trial(wave, potential, sizes_here, owner, local, width, band_count)
            rows = lax.all_to_all(trial, "band", split_axis=0, concat_axis=0, tiled=True)
            rows = rows.reshape(NB, width)
            partial_value = lax.dot_general(
                rows, rows, (((1,), (1,)), ((), ())), preferred_element_type=jnp.float32
            )
            return (jnp.pad(rows, ((0, 0), (0, room - width))), partial_value)

        return branch

    cell_rows, partial_value = lax.switch(
        choice, [forward(width) for width in widths], wave_coeffs[0], old_potential
    )
    gram = summed(partial_value, band_count) * cell_volume
    coeff = newton_schulz(gram)

    def backward(width):
        def branch(cell_rows, coeff):
            fresh = lax.dot_general(
                coeff,
                cell_rows[:, :width],
                (((0,), (0,)), ((), ())),
                preferred_element_type=jnp.float32,
            )
            density = jnp.sum(occupations[0][:, None] * fresh * fresh, axis=0) / NB
            sent = fresh.astype(jnp.bfloat16).reshape(band_count, NB // band_count, width)
            back = lax.all_to_all(sent, "band", split_axis=0, concat_axis=0, tiled=True)
            return (
                unpacked(back, sizes_here, owner, local),
                jnp.pad(density.astype(jnp.bfloat16), (0, room - width)),
            )

        return branch

    waves_out, density = lax.switch(
        choice, [backward(width) for width in widths], cell_rows, coeff
    )
    slab_rows = G // band_count
    slab_start = band_index * slab_rows
    boxes = gathered(density, band_count).astype(jnp.float32)
    whole_box = unpacked(boxes[:, None, :], sizes_here, owner, local)
    padded_x = jnp.pad(whole_box.reshape(BOX, BOX, BOX), ((G, G), (0, 0), (0, 0)))
    planes = lax.dynamic_slice_in_dim(padded_x, slab_start - offsets_here[0] + G, slab_rows, 0)
    frame = jnp.zeros((slab_rows, G + BOX, G + BOX), jnp.float32)
    frame = lax.dynamic_update_slice(frame, planes, (zero_index, offsets_here[1], offsets_here[2]))
    mine = sign_here.astype(jnp.float32) * frame[:, :G, :G]
    patched = lax.psum(mine.astype(jnp.bfloat16), "frag").astype(jnp.float32)
    table, eigen = sine_table()
    spectrum = jnp.einsum("abc,ci->abi", patched, table, precision=highest)
    spectrum = jnp.einsum("abc,bi->aic", spectrum, table, precision=highest)
    columns = lax.all_to_all(
        spectrum.astype(jnp.bfloat16), "band", split_axis=1, concat_axis=0, tiled=True
    ).astype(spectrum.dtype)
    column_count = G // band_count
    eigen_y = lax.dynamic_slice_in_dim(eigen, band_index * column_count, column_count)
    columns = jnp.einsum("abc,ai->ibc", columns, table, precision=highest)
    columns = columns * (
        screening
        / (eigen[:, None, None] + eigen_y[None, :, None] + eigen[None, None, :] + screening)
    )
    columns = jnp.einsum("abc,ai->ibc", columns, table, precision=highest)
    slab = lax.all_to_all(columns, "band", split_axis=0, concat_axis=1, tiled=True)
    slab = jnp.einsum("abc,bi->aic", slab, table, precision=highest)
    hartree = jnp.einsum("abc,ci->abi", slab, table, precision=highest)
    total_potential = hartree - local_factor * jnp.cbrt(jnp.maximum(patched, 0.0))
    grid = lax.all_gather(total_potential.astype(jnp.bfloat16), "band", axis=0, tiled=True).astype(
        total_potential.dtype
    )
    extended = jnp.pad(grid, ((0, BOX), (0, BOX), (0, BOX)))
    window = lax.dynamic_slice(
        extended, (offsets_here[0], offsets_here[1], offsets_here[2]), (BOX, BOX, BOX)
    )
    box_potential = (window.reshape(cells) * mask)[None, :]
    return (waves_out[None], box_potential, total_potential)


def solution(mesh):
    placed = (P("frag", "band", None), P("frag", None), P("frag", None), P(), P(), P())
    return jax.shard_map(
        body,
        mesh=mesh,
        in_specs=placed,
        out_specs=(P("frag", "band", None), P("frag", None), P("band", None, None)),
        check_vma=False,
    )
```
